1024 devices in a mesh: section: 16 (over x, y_hi), hid: 64 (over y_lo, z, core).
Axes of the slice: x: 4, y: 8 (y_hi: 4, y_lo: 2; y = y_hi * 2 + y_lo), z: 16, core: 2. Of those that a mesh axis runs over, the one named last changes fastest.
Arguments:
- layer_input: bfloat16 [16, 256, 4096], P('section', 'hid'), may hold values from -6 to 6
- hidden_grad: bfloat16 [16, 128, 7168], P('section', None, 'hid'), may hold values from -3 to 3
- gate_weight: bfloat16 [16, 4096, 7168], P('section', None, 'hid'), may hold values from -0.09375 to 0.09375
- up_weight: bfloat16 [16, 4096, 7168], P('section', None, 'hid'), may hold values from -0.09375 to 0.09375
- expert_ids: int32 [16, 256, 2], replicated, may hold values from 0 to 7, as said below
Outputs:
- grad_in: bfloat16 [16, 256, 4096], P('section', 'hid')
- grad_gate_weight: bfloat16 [16, 4096, 7168], P('section', None, 'hid')
The draws below stay inside these ranges and needn't reach their ends.
Inputs may be any that keep to these rules, and one draw needn't show every extreme that they name: `expert_ids`: each token names two different experts. In every aligned block of 4 tokens of one section, between 1 and 2 tokens name expert 0; in one section every block has exactly 2.
All inputs are finite; a program needn't handle non-finite values.
Results may differ from the reference program's by a relative error of at most 0.0049.
Values may be sent and summed in bfloat16 or wider, within the bound.
A program may use at most 32 MiB of HBM per device.

```python
import jax
import jax.numpy as jnp
from jax import lax

D = 4096
FF = 7168
EXPERTS = 8
TOK_DEV = 4
K_DEV = 2
TOKENS = 256
CAP = 128
SECTIONS = 16
N_HID = 64


def draw_expert_ids(key, part):
    id_shape = (SECTIONS, TOKENS // TOK_DEV, TOK_DEV)
    count_shape = (SECTIONS, TOKENS // TOK_DEV, 1)
    key_count, key_full, key_order, key_side, key_first, key_pair = jax.random.split(key, 6)
    counts = jax.random.randint(key_count, count_shape, 1, TOK_DEV // 2 + 1)
    full_section = jax.random.randint(key_full, (), 0, SECTIONS)
    section_iota = lax.broadcasted_iota(jnp.int32, count_shape, 0)
    counts = jnp.where(section_iota == full_section, TOK_DEV // 2, counts)
    scores = jax.random.randint(key_order, id_shape, 0, 1 << 20) * TOK_DEV + lax.broadcasted_iota(jnp.int32, id_shape, 2)
    perm_order = jnp.argsort(scores, axis=2)
    token_rank = jnp.argsort(perm_order, axis=2)
    chosen = token_rank < counts
    first_id = jax.random.randint(key_first, id_shape, 1, EXPERTS)
    offset_step = jax.random.randint(key_pair, id_shape, 1, EXPERTS - 1)
    second = 1 + (first_id - 1 + offset_step) % (EXPERTS - 1)
    zero_side = jax.random.randint(key_side, id_shape, 0, 2)
    column_a = jnp.where(chosen & (zero_side == 0), 0, first_id)
    column_b = jnp.where(chosen, jnp.where(zero_side == 0, first_id, 0), second)
    both = jnp.stack([column_a, column_b], axis=-1)
    return both.reshape(SECTIONS, TOKENS, 2).astype(jnp.int32)


def levels(own_key, extent, cuts, low, largest):
    def one(dim, shards_of):
        draws = jax.random.uniform(jax.random.fold_in(jax.random.fold_in(own_key, 6), dim), (shards_of,), jnp.float32, low / len(cuts), largest / len(cuts))
        return jnp.repeat(jnp.exp(draws), extent[dim] // shards_of).reshape((-1,) + (1,) * (len(extent) - dim - 1))

    gain = one(*cuts[0])
    for cut in cuts[1:]:
        gain = gain * one(*cut)
    return gain


def centred(rng, extent, spread, limit, cuts=(), kind=jnp.bfloat16):
    entries = jax.random.normal(rng, extent, jnp.float32) * spread
    if len(cuts) > 0:
        entries = levels(rng, extent, cuts, -0.22, 0.18) * entries
    return jnp.clip(entries, min=-limit, max=limit).astype(kind)


def setup_inputs(seed: int = 0) -> dict:
    seeds = jax.random.split(jax.random.key(seed), 6)
    layer_input = centred(seeds[0], (SECTIONS, TOKENS, D), 1.0, 6.0, ((0, 16), (1, 64)))
    hidden_grad = centred(seeds[1], (SECTIONS, CAP, FF), 0.5, 3.0, ((0, 16), (2, 64)))
    gate_weight = centred(seeds[2], (SECTIONS, D, FF), D ** -0.5, 0.09375, ((0, 16), (2, 64)))
    up_weight = centred(seeds[3], (SECTIONS, D, FF), D ** -0.5, 0.09375, ((0, 16), (2, 64)))
    expert_ids = draw_expert_ids(jax.random.fold_in(seeds[5], 71), 0)
    return dict(layer_input=layer_input, hidden_grad=hidden_grad, gate_weight=gate_weight, up_weight=up_weight, expert_ids=expert_ids)


def slot_index(ids):
    chosen = jnp.any(ids == 0, axis=1).astype(jnp.int32)
    blocks = chosen.reshape(N_HID, TOK_DEV)
    slot_rank = (jnp.cumsum(blocks, axis=1) - blocks).reshape(TOKENS)
    owner_dev = jnp.arange(TOKENS, dtype=jnp.int32) // TOK_DEV
    return jnp.where(chosen == 1, owner_dev * K_DEV + slot_rank, CAP).astype(jnp.int32)


def one_section(inputs, hidden_grad, gate_weight, up_weight, ids):
    slot = slot_index(ids)
    slot_rows = jnp.zeros((CAP + 1, D), jnp.bfloat16).at[slot].set(inputs)[:CAP]
    gate_act = jnp.dot(slot_rows, gate_weight, preferred_element_type=jnp.float32)
    up_act = jnp.dot(slot_rows, up_weight, preferred_element_type=jnp.float32)
    sigmoid_gate = jax.nn.sigmoid(gate_act)
    hidden_float = hidden_grad.astype(jnp.float32)
    grad_gate_act = (hidden_float * up_act * sigmoid_gate * (1.0 + gate_act * (1.0 - sigmoid_gate))).astype(jnp.bfloat16)
    grad_up_act = (hidden_float * gate_act * sigmoid_gate).astype(jnp.bfloat16)
    slot_grad = (jnp.dot(grad_gate_act, gate_weight.T, preferred_element_type=jnp.float32)
                 + jnp.dot(grad_up_act, up_weight.T, preferred_element_type=jnp.float32)).astype(jnp.bfloat16)
    padded = jnp.concatenate([slot_grad, jnp.zeros((1, D), jnp.bfloat16)], axis=0)
    token_grad = padded[slot]
    weight_grad = jnp.dot(slot_rows.T, grad_gate_act, preferred_element_type=jnp.float32).astype(jnp.bfloat16)
    return token_grad, weight_grad


def reference(layer_input, hidden_grad, gate_weight, up_weight, expert_ids):
    token_list = []
    weight_list = []
    for section_num in range(SECTIONS):
        token_grad, weight_grad = one_section(layer_input[section_num], hidden_grad[section_num],
                                            gate_weight[section_num], up_weight[section_num], expert_ids[section_num])
        token_list.append(token_grad)
        weight_list.append(weight_grad)
    grad_in = jnp.roll(jnp.stack(token_list), -1, axis=0)
    return grad_in, jnp.stack(weight_list)
```

```python
import functools

import jax
import jax.numpy as jnp
from jax import lax
from jax.experimental import pallas as pl
from jax.experimental.pallas import tpu as pltpu
from jax.sharding import PartitionSpec as P

MESH = pl.DeviceIdType.MESH
F32 = jnp.float32
BF16 = jnp.bfloat16
Z = 16
ZZ = Z // 2
D = 4096
CH = 8
CW = D // CH
FL = 112


def nt(left, right):
    return lax.dot_general(left, right, (((1,), (1,)), ((), ())), preferred_element_type=F32)


def nn(left, right):
    return lax.dot_general(left, right, (((1,), (0,)), ((), ())), preferred_element_type=F32)


def tn(left, right):
    return lax.dot_general(left, right, (((0,), (0,)), ((), ())), preferred_element_type=F32)


def iota(shape, dim):
    return lax.broadcasted_iota(jnp.int32, shape, dim)


def one_hot(mask):
    return jnp.where(mask, 1.0, 0.0).astype(BF16)


def piece_to_block(i):
    return (i % 8) * 16 + (i // 16) * 2 + (i // 8) % 2


def slots_of(ids_ref, hid_at):
    taken = jnp.int32(0)
    slots = []
    for t in range(4):
        chosen = jnp.where(ids_ref[0, hid_at * 4 + t] * ids_ref[1, hid_at * 4 + t] == 0, 1, 0)
        slots.append(jnp.where(chosen == 1, taken, -1))
        taken = taken + chosen
    return slots


def kernel(
    x_hbm, h_hbm, wg_hbm, wu_hbm, ids_hbm, out_ref, wgrad_hbm,
    xs, hs, wg, wu, ids_a, ids_b, far, rows, hid, gg, part, wgrad,
    s1, r1, s2, r2, s3, r3, s4, r4, s5, r5,
    load_sem, out_sem,
    farg_s, farg_r, nearg_s, nearg_r, yg_s, yg_r, cg_s, cg_r,
    c_s, c_r, y_s, y_r, near_s, near_r, far_s, far_r, pass_s, pass_r,
):
    sec = lax.axis_index("section")
    n_sec = lax.axis_size("section")
    me = lax.axis_index("hid")
    core = me % 2
    z = (me // 2) % Z
    y = me // (2 * Z)
    zz = z // 2
    par = z % 2
    prev_sec = (sec + n_sec - 1) % n_sec
    next_sec = (sec + 1) % n_sec

    def hid_of(y_at, z_at, core_at):
        return (y_at * Z + z_at) * 2 + core_at

    up_z = hid_of(y, (z + 1) % Z, core)
    down_z = hid_of(y, (z + Z - 1) % Z, core)
    other_y = hid_of(1 - y, z, core)
    other_core = hid_of(y, z, 1 - core)
    far_z = [hid_of(y, (z + 2 * k) % Z, core) for k in range(ZZ)]

    def loads(src, dst, i):
        return pltpu.make_async_copy(src, dst, load_sem.at[i])

    def remote(src, dst, send, recv, to, section=None):
        return pltpu.make_async_remote_copy(
            src_ref=src, dst_ref=dst, send_sem=send, recv_sem=recv,
            device_id={"section": sec if section is None else section, "hid": to},
            device_id_type=MESH,
        )

    load_ids = loads(ids_hbm.at[sec], ids_a, 0)
    load_next = loads(ids_hbm.at[next_sec], ids_b, 1)
    load_x = loads(x_hbm.at[0], xs, 2)
    load_h = loads(h_hbm, hs, 3)
    load_wg = loads(wg_hbm, wg, 4)
    load_wu = loads(wu_hbm, wu, 5)
    for c in (load_ids, load_x, load_next, load_h, load_wg, load_wu):
        c.start()

    barrier = pltpu.get_barrier_semaphore()
    peers = far_z[1:] + [up_z, down_z, other_y, other_core]
    for p in peers:
        pl.semaphore_signal(barrier, inc=1, device_id={"section": sec, "hid": p}, device_id_type=MESH)
    pl.semaphore_signal(barrier, inc=1, device_id={"section": next_sec, "hid": me}, device_id_type=MESH)

    load_ids.wait()
    load_x.wait()
    slots = slots_of(ids_a, me)
    row, tok = iota((16, 4), 0), iota((16, 4), 1)
    slot_of_tok = jnp.full((16, 4), -1, jnp.int32)
    for t in range(4):
        slot_of_tok = jnp.where(tok == t, slots[t], slot_of_tok)
    tok_rows = xs[...]
    piece = jnp.zeros((16, CW), F32)
    for j in range(CH):
        pick = one_hot((row // 8 == slot_of_tok) & (row % 8 == j))
        piece += nn(pick, tok_rows[:, j * CW:(j + 1) * CW])
    far[zz] = piece.astype(BF16)

    pl.semaphore_wait(barrier, len(peers) + 1)

    sends = []

    def send(*a, **k):
        c = remote(*a, **k)
        c.start()
        sends.append(c)
        return c

    order = sorted(range(1, ZZ), key=lambda k: -min(k, ZZ - k))
    for k in order:
        send(far.at[zz], far.at[zz], farg_s.at[k - 1], farg_r.at[k - 1], far_z[k])

    load_h.wait()
    m, o = iota((128, 128), 0), iota((128, 128), 1)
    slot_at = ((m // 32) % 2) * 64 + ((m // 2) % 8) * 8 + ((m // 16) % 2) * 4 + (m // 64) * 2 + m % 2
    hid[...] = nt(one_hot(o == slot_at), hs[...]).reshape(4, 32, FL)
    load_wg.wait()
    load_wu.wait()

    for k in order:
        src = (zz + ZZ - k) % ZZ
        remote(far.at[src], far.at[src], farg_s.at[k - 1], farg_r.at[k - 1], far_z[k]).wait_recv()
    to_block = one_hot(m == piece_to_block(o))
    moved = nn(to_block, far[...].reshape(128, CW)).astype(BF16)
    blk = (core * 2 + y) * 2 + par
    blk_p = (core * 2 + y) * 2 + 1 - par
    for j in range(CH):
        rows[blk, :, j * CW:(j + 1) * CW] = moved[j * 16:(j + 1) * 16]

    half = D // 2
    for i, to in ((0, up_z), (1, down_z)):
        cols = pl.ds(i * half, half)
        send(rows.at[blk, :, cols], rows.at[blk, :, cols], nearg_s.at[i], nearg_r.at[i], to)
    send(rows.at[blk], rows.at[blk], yg_s.at[0], yg_r.at[0], other_y)
    send(rows.at[blk], rows.at[blk], cg_s.at[0], cg_r.at[0], other_core)
    for i, to in ((0, up_z), (1, down_z)):
        cols = pl.ds(i * half, half)
        remote(rows.at[blk_p, :, cols], rows.at[blk_p, :, cols], nearg_s.at[i], nearg_r.at[i], to).wait_recv()
    send(rows.at[blk_p], rows.at[blk_p], yg_s.at[1], yg_r.at[1], other_y)
    send(rows.at[blk_p], rows.at[blk_p], cg_s.at[1], cg_r.at[1], other_core)

    def group(core_at, y_at):
        g = core_at * 2 + y_at
        xg = rows[pl.ds(g * 2, 2)].reshape(32, D)
        gate = nt(xg, wg[...])
        up = nt(xg, wu[...])
        sig = 1.0 / (1.0 + jnp.exp(-gate))
        hf = hid[g]
        d_gate = (hf * up * sig * (1.0 + gate * (1.0 - sig))).astype(BF16)
        d_up = (hf * gate * sig).astype(BF16)
        gg[g] = d_gate
        part[pl.ds(g * 2, 2)] = (nn(d_gate, wg[...]) + nn(d_up, wu[...])).reshape(2, 16, D)

    group(core, y)
    yblk = (core * 2 + 1 - y) * 2 + par
    yblk_p = (core * 2 + 1 - y) * 2 + 1 - par
    remote(rows.at[yblk], rows.at[yblk], yg_s.at[0], yg_r.at[0], other_y).wait_recv()
    send(rows.at[yblk], rows.at[yblk], cg_s.at[2], cg_r.at[2], other_core)
    remote(rows.at[yblk_p], rows.at[yblk_p], yg_s.at[1], yg_r.at[1], other_y).wait_recv()
    send(rows.at[yblk_p], rows.at[yblk_p], cg_s.at[3], cg_r.at[3], other_core)

    def from_core(i, y_at, par_at):
        b = ((1 - core) * 2 + y_at) * 2 + par_at
        remote(rows.at[b], rows.at[b], cg_s.at[i], cg_r.at[i], other_core).wait_recv()

    def to_core(i, y_at, par_at):
        b = ((1 - core) * 2 + y_at) * 2 + par_at
        s1[i] = part[b].astype(BF16)
        send(s1.at[i], r1.at[i], c_s.at[i], c_r.at[i], other_core)

    group(core, 1 - y)
    from_core(0, y, par)
    from_core(1, y, 1 - par)
    group(1 - core, y)
    from_core(2, 1 - y, par)
    from_core(3, 1 - y, 1 - par)
    group(1 - core, 1 - y)
    to_core(0, 1 - y, 1 - par)
    to_core(1, 1 - y, par)
    to_core(2, y, 1 - par)
    to_core(3, y, par)

    def core_sum(i, y_at, par_at):
        remote(s1.at[i], r1.at[i], c_s.at[i], c_r.at[i], other_core).wait_recv()
        b = (core * 2 + y_at) * 2 + par_at
        return part[b] + r1[i].astype(F32)

    for i, par_at in ((0, 1 - par), (1, par)):
        s2[i] = core_sum(i, 1 - y, par_at).astype(BF16)
        send(s2.at[i], r2.at[i], y_s.at[i], y_r.at[i], other_y)
    part[blk_p] = core_sum(2, y, 1 - par)
    part[blk] = core_sum(3, y, par)

    all_gg = gg[...].reshape(128, FL)
    for j in range(CH):
        cols = slice(j * CW, (j + 1) * CW)
        wgrad[:, cols] = tn(all_gg, rows[:, :, cols].reshape(128, CW)).astype(BF16)
    store = pltpu.make_async_copy(wgrad, wgrad_hbm, out_sem)
    store.start()

    remote(s2.at[0], r2.at[0], y_s.at[0], y_r.at[0], other_y).wait_recv()
    s3[...] = (part[blk_p] + r2[0].astype(F32)).astype(BF16)
    for i, to in ((0, up_z), (1, down_z)):
        cols = pl.ds(i * half, half)
        send(s3.at[:, cols], r3.at[:, cols], near_s.at[i], near_r.at[i], to)
    remote(s2.at[1], r2.at[1], y_s.at[1], y_r.at[1], other_y).wait_recv()
    own = part[blk] + r2[1].astype(F32)
    for i, to in ((0, up_z), (1, down_z)):
        cols = pl.ds(i * half, half)
        remote(s3.at[:, cols], r3.at[:, cols], near_s.at[i], near_r.at[i], to).wait_recv()
    own = (own + r3[...].astype(F32)).astype(BF16)
    to_piece = one_hot(o == piece_to_block(m))
    stacked = jnp.concatenate([own[:, j * CW:(j + 1) * CW] for j in range(CH)], axis=0)
    s4[...] = nn(to_piece, stacked).astype(BF16).reshape(ZZ, 16, CW)
    for k in order:
        to = (zz + k) % ZZ
        send(s4.at[to], r4.at[k - 1], far_s.at[k - 1], far_r.at[k - 1], far_z[k])
    total = s4[zz].astype(F32)
    for k in order:
        remote(s4.at[zz], r4.at[k - 1], far_s.at[k - 1], far_r.at[k - 1], far_z[k]).wait_recv()
        total += r4[k - 1].astype(F32)
    s5[...] = total.astype(BF16)
    send(s5, r5, pass_s, pass_r, me, section=prev_sec)

    load_next.wait()
    slots_n = slots_of(ids_b, me)
    trow, tcol = iota((4, 16), 0), iota((4, 16), 1)
    slot_of_row = jnp.full((4, 16), -1, jnp.int32)
    for t in range(4):
        slot_of_row = jnp.where(trow == t, slots_n[t], slot_of_row)
    store.wait()
    for c in sends[:-1]:
        c.wait_send()
    sends[-1].wait()
    got = r5[...]
    for j in range(CH):
        pick = one_hot((tcol // 8 == slot_of_row) & (tcol % 8 == j))
        out_ref[0, :, j * CW:(j + 1) * CW] = nn(pick, got).astype(BF16)


def per_device(layer_input, hidden_grad, gate_weight, up_weight, expert_ids):
    dma = pltpu.SemaphoreType.DMA
    anywhere = pl.BlockSpec(memory_space=pl.ANY)
    out, wgrad = pl.pallas_call(
        kernel,
        out_shape=(
            jax.ShapeDtypeStruct((1, 4, D), BF16),
            jax.ShapeDtypeStruct((FL, D), BF16),
        ),
        in_specs=[anywhere] * 5,
        out_specs=(pl.BlockSpec(memory_space=pltpu.VMEM), anywhere),
        scratch_shapes=[
            pltpu.VMEM((4, D), BF16),
            pltpu.VMEM((FL, 128), BF16),
            pltpu.VMEM((FL, D), BF16),
            pltpu.VMEM((FL, D), BF16),
            pltpu.SMEM((2, 256), jnp.int32),
            pltpu.SMEM((2, 256), jnp.int32),
            pltpu.VMEM((ZZ, 16, CW), BF16),
            pltpu.VMEM((8, 16, D), BF16),
            pltpu.VMEM((4, 32, FL), F32),
            pltpu.VMEM((4, 32, FL), BF16),
            pltpu.VMEM((8, 16, D), F32),
            pltpu.VMEM((FL, D), BF16),
            pltpu.VMEM((4, 16, D), BF16),
            pltpu.VMEM((4, 16, D), BF16),
            pltpu.VMEM((2, 16, D), BF16),
            pltpu.VMEM((2, 16, D), BF16),
            pltpu.VMEM((16, D), BF16),
            pltpu.VMEM((16, D), BF16),
            pltpu.VMEM((ZZ, 16, CW), BF16),
            pltpu.VMEM((ZZ - 1, 16, CW), BF16),
            pltpu.VMEM((16, CW), BF16),
            pltpu.VMEM((16, CW), BF16),
            dma((6,)),
            dma,
            dma((ZZ - 1,)), dma((ZZ - 1,)),
            dma((2,)), dma((2,)),
            dma((2,)), dma((2,)),
            dma((4,)), dma((4,)),
            dma((4,)), dma((4,)),
            dma((2,)), dma((2,)),
            dma((2,)), dma((2,)),
            dma((ZZ - 1,)), dma((ZZ - 1,)),
            dma, dma,
        ],
        compiler_params=pltpu.CompilerParams(
            collective_id=0, has_side_effects=True, vmem_limit_bytes=60 * 2**20
        ),
        name="relay",
    )(
        layer_input,
        jnp.swapaxes(hidden_grad[0], 0, 1),
        jnp.swapaxes(gate_weight[0], 0, 1),
        jnp.swapaxes(up_weight[0], 0, 1),
        jnp.swapaxes(expert_ids, 1, 2),
    )
    return out, jnp.swapaxes(wgrad, 0, 1)[None]


def solution(mesh):
    return jax.shard_map(
        per_device,
        mesh=mesh,
        in_specs=(
            P("section", "hid", None),
            P("section", None, "hid"),
            P("section", None, "hid"),
            P("section", None, "hid"),
            P(),
        ),
        out_specs=(P("section", "hid", None), P("section", None, "hid")),
        check_vma=False,
    )
```

```python
import functools

import jax
import jax.numpy as jnp
from jax import lax
from jax.experimental import pallas as pl
from jax.experimental.pallas import tpu as pltpu
from jax.sharding import PartitionSpec as P

MESH = pl.DeviceIdType.MESH
F32 = jnp.float32
BF16 = jnp.bfloat16
Z = 16
D = 4096
CH = 8
CW = D // CH
FL = 112

DISTANCES = tuple(range(1 - Z // 2, Z // 2 + 1))
FIRST, EACH, Y_TRIP, SLOT = 1.4, 0.6, 2.1, 0.28


def both_ways(tree):
    back = {-d: -p for d, p in tree.items() if d < Z // 2}
    return {**tree, **back}


GATHER_FROM = both_ways({1: 0, 2: 1, 3: 2, 4: 0, 5: 4, 6: 4, 7: 4, 8: 4})
SUM_FROM = both_ways({1: 0, 2: 0, 3: 0, 4: 0, 5: 4, 6: 2, 7: 4, 8: 4})


def trip(tree, d):
    return 0.0 if d == 0 else FIRST + EACH * abs(d - tree[d]) + trip(tree, tree[d])


def below(tree, d):
    return [c for c in tree if tree[c] == d]


def deepest(tree, d, top):
    return max([trip(tree, d)] + [deepest(tree, c, top) for c in below(tree, d)]) - (trip(tree, d) if top else 0.0)


def far_first(tree, d):
    return sorted(below(tree, d), key=lambda c: (-max(deepest(tree, c, False), trip(tree, c)), -abs(c), c))


GATHER_TO = {d: far_first(GATHER_FROM, d) for d in DISTANCES}
GATHER_ORDER = [
    (own, d)
    for _, own, d in sorted(
        [(trip(GATHER_FROM, d), True, d) for d in DISTANCES if d != 0]
        + [(trip(GATHER_FROM, d) + Y_TRIP, False, d) for d in DISTANCES]
    )
]
SUM_TO = {d: below(SUM_FROM, d) for d in DISTANCES}
SUM_Y_ORDER = sorted(DISTANCES, key=lambda d: (-trip(SUM_FROM, d), d))


def sum_ready(d):
    at = Y_TRIP + SLOT * SUM_Y_ORDER.index(d)
    return max([at] + [sum_ready(c) + FIRST + EACH * abs(c - d) for c in SUM_TO[d]])


SUM_Z_ORDER = sorted(DISTANCES, key=lambda d: (d == 0, sum_ready(d)))
REACH = sorted(
    {s * (d - tree[d]) for tree in (GATHER_FROM, SUM_FROM) for d in tree for s in (1, -1)}
)


def nt(left, right):
    return lax.dot_general(left, right, (((1,), (1,)), ((), ())), preferred_element_type=F32)


def nn(left, right):
    return lax.dot_general(left, right, (((1,), (0,)), ((), ())), preferred_element_type=F32)


def tn(left, right):
    return lax.dot_general(left, right, (((0,), (0,)), ((), ())), preferred_element_type=F32)


def iota(shape, dim):
    return lax.broadcasted_iota(jnp.int32, shape, dim)


def one_hot(mask):
    return jnp.where(mask, 1.0, 0.0).astype(BF16)


def piece_to_block(i):
    return (i % 8) * 16 + (i // 16) * 2 + (i // 8) % 2


def slots_of(ids_ref, hid_at):
    taken = jnp.int32(0)
    slots = []
    for t in range(4):
        chosen = jnp.where(ids_ref[0, hid_at * 4 + t] * ids_ref[1, hid_at * 4 + t] == 0, 1, 0)
        slots.append(jnp.where(chosen == 1, taken, -1))
        taken = taken + chosen
    return slots


def kernel(
    x_hbm, h_hbm, wg_hbm, wu_hbm, ids_hbm, out_ref, wgrad_hbm,
    xs, hs, wg, wu, ids_a, ids_b, got, rows, hid, part, wgrad,
    mine, core_in, y_out, y_in, acc, z_out, z_in, s5, r5,
    load_sem, out_sem,
    got_r, gz_s, gy_s, gcore_s, c_s, c_r, y_s, y_r, z_s, z_r, pass_s, pass_r,
):
    sec = lax.axis_index("section")
    n_sec = lax.axis_size("section")
    me = lax.axis_index("hid")
    core = me % 2
    z = (me // 2) % Z
    y = me // (2 * Z)
    prev_sec = (sec + n_sec - 1) % n_sec
    next_sec = (sec + 1) % n_sec

    def hid_of(y_at, z_at, core_at):
        return (y_at * Z + z_at) * 2 + core_at

    other_y = hid_of(1 - y, z, core)
    other_core = hid_of(y, z, 1 - core)

    def along(d):
        return (z + d + Z) % Z

    def loads(src, dst, i):
        return pltpu.make_async_copy(src, dst, load_sem.at[i])

    def remote(src, dst, send, recv, to, section=None):
        return pltpu.make_async_remote_copy(
            src_ref=src, dst_ref=dst, send_sem=send, recv_sem=recv,
            device_id={"section": sec if section is None else section, "hid": to},
            device_id_type=MESH,
        )

    load_ids = loads(ids_hbm.at[sec], ids_a, 0)
    load_next = loads(ids_hbm.at[next_sec], ids_b, 1)
    load_x = loads(x_hbm.at[0], xs, 2)
    load_h = loads(h_hbm, hs, 3)
    load_wg = loads(wg_hbm, wg, 4)
    load_wu = loads(wu_hbm, wu, 5)
    for c in (load_ids, load_x, load_next, load_h, load_wg, load_wu):
        c.start()

    barrier = pltpu.get_barrier_semaphore()
    peers = [hid_of(y, along(d), core) for d in REACH] + [other_y, other_core]
    for p in peers:
        pl.semaphore_signal(barrier, inc=1, device_id={"section": sec, "hid": p}, device_id_type=MESH)
    pl.semaphore_signal(barrier, inc=1, device_id={"section": next_sec, "hid": me}, device_id_type=MESH)

    load_ids.wait()
    load_x.wait()
    slots = slots_of(ids_a, me)
    row, tok = iota((16, 4), 0), iota((16, 4), 1)
    slot_of_tok = jnp.full((16, 4), -1, jnp.int32)
    for t in range(4):
        slot_of_tok = jnp.where(tok == t, slots[t], slot_of_tok)
    tok_rows = xs[...]
    piece = jnp.zeros((16, CW), F32)
    for j in range(CH):
        pick = one_hot((row // 8 == slot_of_tok) & (row % 8 == j))
        piece += nn(pick, tok_rows[:, j * CW:(j + 1) * CW])
    got[core, z, y] = piece.astype(BF16)

    pl.semaphore_wait(barrier, len(peers) + 1)

    sends = []

    def send(*a, **k):
        c = remote(*a, **k)
        c.start()
        sends.append(c)

    def pass_on(core_at, d, y_at, sem, to):
        ref = got.at[core_at, along(-d), y_at]
        return remote(ref, ref, sem, got_r.at[core_at, along(-d), y_at], to)

    def landed(core_at, d, y_at):
        pass_on(core_at, d, y_at, gcore_s.at[0], other_core).wait_recv()

    def send_on(copy):
        copy.start()
        sends.append(copy)

    def own_side(d):
        for to in GATHER_TO[d]:
            send_on(pass_on(core, d, y, gz_s.at[to + Z // 2 - 1], hid_of(y, along(to - d), core)))
        i = d + Z // 2 - 1
        send_on(pass_on(core, d, y, gy_s.at[i], other_y))
        send_on(pass_on(core, d, y, gcore_s.at[i], other_core))

    def other_side(d):
        landed(core, d, 1 - y)
        send_on(pass_on(core, d, 1 - y, gcore_s.at[Z + d + Z // 2 - 1], other_core))

    own_side(0)

    load_h.wait()
    m, o = iota((128, 128), 0), iota((128, 128), 1)
    slot_at = ((m // 16) % 2) * 64 + ((m // 32) % 2) * 32 + ((m // 2) % 8) * 4 + (m // 64) * 2 + m % 2
    hid[...] = nt(one_hot(o == slot_at), hs[...])

    for is_own, d in GATHER_ORDER:
        if is_own:
            landed(core, d, y)
            own_side(d)
        else:
            other_side(d)

    to_block = one_hot(m == piece_to_block(o))

    def unpack(core_at):
        for o_z in range(2):
            for y_at in range(2):
                moved = nn(to_block, got[core_at, o_z * 8:o_z * 8 + 8, y_at].reshape(128, CW)).astype(BF16)
                b = (core_at * 2 + o_z) * 2 + y_at
                for j in range(CH):
                    rows[b, :, j * CW:(j + 1) * CW] = moved[j * 16:(j + 1) * 16]

    unpack(core)
    for d in DISTANCES:
        for y_at in range(2):
            landed(1 - core, d, y_at)
    unpack(1 - core)

    load_wg.wait()
    load_wu.wait()
    all_rows = rows[...].reshape(128, D)
    gate = nt(all_rows, wg[...])
    up = nt(all_rows, wu[...])
    sig = 1.0 / (1.0 + jnp.exp(-gate))
    hf = hid[...]
    d_gate = (hf * up * sig * (1.0 + gate * (1.0 - sig))).astype(BF16)
    d_up = (hf * gate * sig).astype(BF16)
    to_piece = one_hot(o == piece_to_block(m))
    part[...] = (nn(d_gate, wg[...]) + nn(d_up, wu[...])).astype(BF16).reshape(8, 16, D)

    def repack(core_at):
        for o_z in range(2):
            for y_at in range(2):
                own = part[(core_at * 2 + o_z) * 2 + y_at]
                stacked = jnp.concatenate([own[:, j * CW:(j + 1) * CW] for j in range(CH)], axis=0)
                moved = nn(to_piece, stacked).astype(BF16).reshape(8, 16, CW)
                mine[core_at, o_z * 8:o_z * 8 + 8, y_at] = moved

    def core_copy(i, d):
        return remote(mine.at[1 - core, along(-d)], core_in.at[i], c_s.at[i], c_r.at[i], other_core)

    def y_copy(i):
        return remote(y_out.at[i], y_in.at[i], y_s.at[i], y_r.at[i], other_y)

    def z_copy(d):
        i = d + Z // 2 - 1
        return remote(z_out.at[i], z_in.at[i], z_s.at[i], z_r.at[i], hid_of(y, along(SUM_FROM[d] - d), core))

    repack(1 - core)
    for i, d in enumerate(SUM_Y_ORDER):
        send_on(core_copy(i, d))
    repack(core)
    for i, d in enumerate(SUM_Y_ORDER):
        core_copy(i, d).wait_recv()
        at = along(-d)
        y_out[i] = (mine[core, at, 1 - y].astype(F32) + core_in[i, 1 - y].astype(F32)).astype(BF16)
        send_on(y_copy(i))
        acc[i] = mine[core, at, y].astype(F32) + core_in[i, y].astype(F32)
    for d in SUM_Z_ORDER:
        i = SUM_Y_ORDER.index(d)
        y_copy(i).wait_recv()
        total = acc[i] + y_in[i].astype(F32)
        for child in SUM_TO[d]:
            z_copy(child).wait_recv()
            total += z_in[child + Z // 2 - 1].astype(F32)
        if d != 0:
            z_out[d + Z // 2 - 1] = total.astype(BF16)
            send_on(z_copy(d))
    s5[...] = total.astype(BF16)
    send(s5, r5, pass_s, pass_r, me, section=prev_sec)

    for j in range(CH):
        cols = slice(j * CW, (j + 1) * CW)
        wgrad[:, cols] = tn(d_gate, rows[:, :, cols].reshape(128, CW)).astype(BF16)
    store = pltpu.make_async_copy(wgrad, wgrad_hbm, out_sem)
    store.start()
    load_next.wait()
    slots_n = slots_of(ids_b, me)
    trow, tcol = iota((4, 16), 0), iota((4, 16), 1)
    slot_of_row = jnp.full((4, 16), -1, jnp.int32)
    for t in range(4):
        slot_of_row = jnp.where(trow == t, slots_n[t], slot_of_row)
    store.wait()
    for c in sends[:-1]:
        c.wait_send()
    sends[-1].wait()
    last = r5[...]
    for j in range(CH):
        pick = one_hot((tcol // 8 == slot_of_row) & (tcol % 8 == j))
        out_ref[0, :, j * CW:(j + 1) * CW] = nn(pick, last).astype(BF16)


def per_device(layer_input, hidden_grad, gate_weight, up_weight, expert_ids):
    dma = pltpu.SemaphoreType.DMA
    anywhere = pl.BlockSpec(memory_space=pl.ANY)
    out, wgrad = pl.pallas_call(
        kernel,
        out_shape=(
            jax.ShapeDtypeStruct((1, 4, D), BF16),
            jax.ShapeDtypeStruct((FL, D), BF16),
        ),
        in_specs=[anywhere] * 5,
        out_specs=(pl.BlockSpec(memory_space=pltpu.VMEM), anywhere),
        scratch_shapes=[
            pltpu.VMEM((4, D), BF16),
            pltpu.VMEM((FL, 128), BF16),
            pltpu.VMEM((FL, D), BF16),
            pltpu.VMEM((FL, D), BF16),
            pltpu.SMEM((2, 256), jnp.int32),
            pltpu.SMEM((2, 256), jnp.int32),
            pltpu.VMEM((2, Z, 2, 16, CW), BF16),
            pltpu.VMEM((8, 16, D), BF16),
            pltpu.VMEM((128, FL), F32),
            pltpu.VMEM((8, 16, D), BF16),
            pltpu.VMEM((FL, D), BF16),
            pltpu.VMEM((2, Z, 2, 16, CW), BF16),
            pltpu.VMEM((16, 2, 16, CW), BF16),
            pltpu.VMEM((16, 16, CW), BF16),
            pltpu.VMEM((16, 16, CW), BF16),
            pltpu.VMEM((16, 16, CW), F32),
            pltpu.VMEM((Z, 16, CW), BF16),
            pltpu.VMEM((Z, 16, CW), BF16),
            pltpu.VMEM((16, CW), BF16),
            pltpu.VMEM((16, CW), BF16),
            dma((6,)),
            dma,
            dma((2, Z, 2)),
            dma((Z,)), dma((Z,)), dma((2 * Z,)),
            dma((Z,)), dma((Z,)),
            dma((Z,)), dma((Z,)),
            dma((Z,)), dma((Z,)),
            dma, dma,
        ],
        compiler_params=pltpu.CompilerParams(
            collective_id=0, has_side_effects=True, vmem_limit_bytes=60 * 2**20
        ),
        name="relay",
    )(
        layer_input,
        jnp.swapaxes(hidden_grad[0], 0, 1),
        jnp.swapaxes(gate_weight[0], 0, 1),
        jnp.swapaxes(up_weight[0], 0, 1),
        jnp.swapaxes(expert_ids, 1, 2),
    )
    return out, jnp.swapaxes(wgrad, 0, 1)[None]


def solution(mesh):
    return jax.shard_map(
        per_device,
        mesh=mesh,
        in_specs=(
            P("section", "hid", None),
            P("section", None, "hid"),
            P("section", None, "hid"),
            P("section", None, "hid"),
            P(),
        ),
        out_specs=(P("section", "hid", None), P("section", None, "hid")),
        check_vma=False,
    )
```

```python
import functools

import jax
import jax.numpy as jnp
from jax import lax
from jax.experimental import pallas as pl
from jax.experimental.pallas import tpu as pltpu
from jax.sharding import PartitionSpec as P

MESH = pl.DeviceIdType.MESH
F32 = jnp.float32
BF16 = jnp.bfloat16
Z = 16
D = 4096
CH = 8
CW = D // CH
FL = 112
PARTS = 7

DISTANCES = tuple(range(1 - Z // 2, Z // 2 + 1))
FIRST, EACH, Y_TRIP, SLOT = 1.4, 0.6, 2.1, 0.28


def both_ways(tree):
    back = {-d: -p for d, p in tree.items() if d < Z // 2}
    return {**tree, **back}


GATHER_FROM = both_ways({1: 0, 2: 1, 3: 2, 4: 0, 5: 4, 6: 4, 7: 4, 8: 4})
SUM_FROM = both_ways({1: 0, 2: 0, 3: 0, 4: 2, 5: 2, 6: 0, 7: 6, 8: 6})


def trip(tree, d):
    return 0.0 if d == 0 else FIRST + EACH * abs(d - tree[d]) + trip(tree, tree[d])


def below(tree, d):
    return [c for c in tree if tree[c] == d]


def deepest(tree, d, top):
    return max([trip(tree, d)] + [deepest(tree, c, top) for c in below(tree, d)]) - (trip(tree, d) if top else 0.0)


def far_first(tree, d):
    return sorted(below(tree, d), key=lambda c: (-max(deepest(tree, c, False), trip(tree, c)), -abs(c), c))


GATHER_TO = {d: far_first(GATHER_FROM, d) for d in DISTANCES}
GATHER_ORDER = [
    (own, d)
    for _, own, d in sorted(
        [(trip(GATHER_FROM, d), True, d) for d in DISTANCES if d != 0]
        + [(trip(GATHER_FROM, d) + Y_TRIP, False, d) for d in DISTANCES]
    )
]
SUM_TO = {d: below(SUM_FROM, d) for d in DISTANCES}
SUM_Y_ORDER = sorted(DISTANCES, key=lambda d: (-trip(SUM_FROM, d), d))


def sum_ready(d):
    at = Y_TRIP + SLOT * SUM_Y_ORDER.index(d)
    return max([at] + [sum_ready(c) + FIRST + EACH * abs(c - d) for c in SUM_TO[d]])


SUM_Z_ORDER = sorted(DISTANCES, key=lambda d: (d == 0, sum_ready(d)))
REACH = sorted({s * (d - p) for d, p in GATHER_FROM.items() for s in (1, -1)})


def nt(left, right):
    return lax.dot_general(left, right, (((1,), (1,)), ((), ())), preferred_element_type=F32)


def nn(left, right):
    return lax.dot_general(left, right, (((1,), (0,)), ((), ())), preferred_element_type=F32)


def tn(left, right):
    return lax.dot_general(left, right, (((0,), (0,)), ((), ())), preferred_element_type=F32)


def iota(shape, dim):
    return lax.broadcasted_iota(jnp.int32, shape, dim)


def one_hot(mask):
    return jnp.where(mask, 1.0, 0.0).astype(BF16)


def piece_to_block(i):
    return (i % 8) * 16 + (i // 16) * 2 + (i // 8) % 2


def slots_of(ids_ref, hid_at):
    taken = jnp.int32(0)
    slots = []
    for t in range(4):
        chosen = jnp.where(ids_ref[0, hid_at * 4 + t] * ids_ref[1, hid_at * 4 + t] == 0, 1, 0)
        slots.append(jnp.where(chosen == 1, taken, -1))
        taken = taken + chosen
    return slots


def kernel(
    x_hbm, h_hbm, wg_hbm, wu_hbm, ids_hbm, got_out, wgrad_hbm,
    xs, hs, wg, wu, ids_a, got, rows, hid, part, wgrad,
    mine, core_in, y_out, y_in, acc, z_out, z_in, s5,
    load_sem, out_sem,
    got_r, gz_s, gy_s, gcore_s, c_s, c_r, y_s, y_r, z_s, z_r, pass_s, pass_r,
):
    sec = lax.axis_index("section")
    n_sec = lax.axis_size("section")
    me = lax.axis_index("hid")
    core = me % 2
    z = (me // 2) % Z
    y = me // (2 * Z)
    prev_sec = (sec + n_sec - 1) % n_sec
    next_sec = (sec + 1) % n_sec

    def hid_of(y_at, z_at, core_at):
        return (y_at * Z + z_at) * 2 + core_at

    other_y = hid_of(1 - y, z, core)
    other_core = hid_of(y, z, 1 - core)

    def along(d):
        return (z + d + Z) % Z

    def loads(src, dst, i):
        return pltpu.make_async_copy(src, dst, load_sem.at[i])

    def remote(src, dst, send, recv, to, section=None):
        return pltpu.make_async_remote_copy(
            src_ref=src, dst_ref=dst, send_sem=send, recv_sem=recv,
            device_id={"section": sec if section is None else section, "hid": to},
            device_id_type=MESH,
        )

    load_ids = loads(ids_hbm.at[sec], ids_a, 0)
    load_x = loads(x_hbm.at[0], xs, 2)
    load_h = loads(h_hbm, hs, 3)
    load_wg = loads(wg_hbm, wg, 4)
    load_wu = loads(wu_hbm, wu, 5)
    for c in (load_ids, load_x, load_h, load_wg, load_wu):
        c.start()

    barrier = pltpu.get_barrier_semaphore()
    peers = [hid_of(y, along(d), core) for d in REACH] + [other_y, other_core]
    for p in peers:
        pl.semaphore_signal(barrier, inc=1, device_id={"section": sec, "hid": p}, device_id_type=MESH)
    pl.semaphore_signal(barrier, inc=1, device_id={"section": next_sec, "hid": me}, device_id_type=MESH)

    load_ids.wait()
    load_x.wait()
    slots = slots_of(ids_a, me)
    row, tok = iota((16, 4), 0), iota((16, 4), 1)
    slot_of_tok = jnp.full((16, 4), -1, jnp.int32)
    for t in range(4):
        slot_of_tok = jnp.where(tok == t, slots[t], slot_of_tok)
    tok_rows = xs[...]
    piece = jnp.zeros((16, CW), F32)
    for j in range(CH):
        pick = one_hot((row // 8 == slot_of_tok) & (row % 8 == j))
        piece += nn(pick, tok_rows[:, j * CW:(j + 1) * CW])
    got[core, z, y] = piece.astype(BF16)

    pl.semaphore_wait(barrier, len(peers) + 1)

    sends = []

    def send(*a, **k):
        c = remote(*a, **k)
        c.start()
        sends.append(c)

    def pass_on(core_at, d, y_at, sem, to):
        ref = got.at[core_at, along(-d), y_at]
        return remote(ref, ref, sem, got_r.at[core_at, along(-d), y_at], to)

    def landed(core_at, d, y_at):
        pass_on(core_at, d, y_at, gcore_s.at[0], other_core).wait_recv()

    def send_on(copy):
        copy.start()
        sends.append(copy)

    def own_side(d):
        for to in GATHER_TO[d]:
            send_on(pass_on(core, d, y, gz_s.at[to + Z // 2 - 1], hid_of(y, along(to - d), core)))
        i = d + Z // 2 - 1
        send_on(pass_on(core, d, y, gy_s.at[i], other_y))
        send_on(pass_on(core, d, y, gcore_s.at[i], other_core))

    def other_side(d):
        landed(core, d, 1 - y)
        send_on(pass_on(core, d, 1 - y, gcore_s.at[Z + d + Z // 2 - 1], other_core))

    own_side(0)

    load_h.wait()
    m, o = iota((128, 128), 0), iota((128, 128), 1)
    slot_at = ((m // 16) % 2) * 64 + ((m // 32) % 2) * 32 + ((m // 2) % 8) * 4 + (m // 64) * 2 + m % 2
    hid[...] = nt(one_hot(o == slot_at), hs[...])

    for is_own, d in GATHER_ORDER:
        if is_own:
            landed(core, d, y)
            own_side(d)
        else:
            other_side(d)

    to_block = one_hot(m == piece_to_block(o))

    def unpack(core_at):
        for o_z in range(2):
            for y_at in range(2):
                moved = nn(to_block, got[core_at, o_z * 8:o_z * 8 + 8, y_at].reshape(128, CW)).astype(BF16)
                b = (core_at * 2 + o_z) * 2 + y_at
                for j in range(CH):
                    rows[b, :, j * CW:(j + 1) * CW] = moved[j * 16:(j + 1) * 16]

    unpack(core)
    for d in DISTANCES:
        for y_at in range(2):
            landed(1 - core, d, y_at)
    unpack(1 - core)

    load_wg.wait()
    load_wu.wait()
    all_rows = rows[...].reshape(128, D)
    gate = nt(all_rows, wg[...])
    up = nt(all_rows, wu[...])
    sig = 1.0 / (1.0 + jnp.exp(-gate))
    hf = hid[...]
    d_gate = (hf * up * sig * (1.0 + gate * (1.0 - sig))).astype(BF16)
    d_up = (hf * gate * sig).astype(BF16)
    to_piece = one_hot(o == piece_to_block(m))
    part[...] = (nn(d_gate, wg[...]) + nn(d_up, wu[...])).astype(BF16).reshape(8, 16, D)

    def repack(core_at):
        for o_z in range(2):
            for y_at in range(2):
                own = part[(core_at * 2 + o_z) * 2 + y_at]
                stacked = jnp.concatenate([own[:, j * CW:(j + 1) * CW] for j in range(CH)], axis=0)
                moved = nn(to_piece, stacked).astype(BF16).reshape(8, 16, CW)
                mine[core_at, o_z * 8:o_z * 8 + 8, y_at] = moved

    def core_copy(i, d):
        return remote(mine.at[1 - core, along(-d)], core_in.at[i], c_s.at[i], c_r.at[i], other_core)

    def y_copy(i):
        return remote(y_out.at[i], y_in.at[i], y_s.at[i], y_r.at[i], other_y)

    def z_copy(d):
        i = d + Z // 2 - 1
        return remote(z_out.at[i], z_in.at[i], z_s.at[i], z_r.at[i], hid_of(y, along(SUM_FROM[d] - d), core))

    repack(1 - core)
    for i, d in enumerate(SUM_Y_ORDER):
        send_on(core_copy(i, d))
    repack(core)
    for i, d in enumerate(SUM_Y_ORDER):
        core_copy(i, d).wait_recv()
        at = along(-d)
        y_out[i] = (mine[core, at, 1 - y].astype(F32) + core_in[i, 1 - y].astype(F32)).astype(BF16)
        send_on(y_copy(i))
        acc[i] = mine[core, at, y].astype(F32) + core_in[i, y].astype(F32)
    for d in SUM_Z_ORDER:
        i = SUM_Y_ORDER.index(d)
        y_copy(i).wait_recv()
        total = acc[i] + y_in[i].astype(F32)
        for child in SUM_TO[d]:
            z_copy(child).wait_recv()
            total += z_in[child + Z // 2 - 1].astype(F32)
        if d != 0:
            z_out[d + Z // 2 - 1] = total.astype(BF16)
            send_on(z_copy(d))
    s5[...] = total.astype(BF16)
    send(s5, got_out, pass_s, pass_r, me, section=prev_sec)

    for j in range(CH):
        cols = slice(j * CW, (j + 1) * CW)
        wgrad[:, cols] = tn(d_gate, rows[:, :, cols].reshape(128, CW)).astype(BF16)
    store = pltpu.make_async_copy(wgrad, wgrad_hbm, out_sem)
    store.start()
    store.wait()
    for c in sends[:-1]:
        c.wait_send()
    sends[-1].wait()


def finish(ids_hbm, got_hbm, wgrad_in, out_hbm, wgrad_out, ids, last_ref, tokens, held, sems, out_sems):
    me = lax.axis_index("hid")
    next_sec = (lax.axis_index("section") + 1) % lax.axis_size("section")
    load = pltpu.make_async_copy(ids_hbm.at[next_sec], ids, sems.at[0])
    load.start()
    load_last = pltpu.make_async_copy(got_hbm, last_ref, sems.at[1 + PARTS])
    load_last.start()
    step = FL // PARTS
    moves = []
    for i in range(PARTS):
        part = pl.ds(i * step, step)
        moves.append((
            pltpu.make_async_copy(wgrad_in.at[part], held.at[part], sems.at[1 + i]),
            pltpu.make_async_copy(held.at[part], wgrad_out.at[part], out_sems.at[i]),
        ))
        moves[-1][0].start()
    load.wait()
    slots = slots_of(ids, me)
    row, col = iota((4, 16), 0), iota((4, 16), 1)
    slot_of_row = jnp.full((4, 16), -1, jnp.int32)
    for t in range(4):
        slot_of_row = jnp.where(row == t, slots[t], slot_of_row)
    load_last.wait()
    last = last_ref[...]
    for j in range(CH):
        pick = one_hot((col // 8 == slot_of_row) & (col % 8 == j))
        tokens[:, j * CW:(j + 1) * CW] = nn(pick, last).astype(BF16)
    store = pltpu.make_async_copy(tokens, out_hbm.at[0], out_sems.at[PARTS])
    store.start()
    for come, go in moves:
        come.wait()
        go.start()
    for _, go in moves:
        go.wait()
    store.wait()


def per_device(layer_input, hidden_grad, gate_weight, up_weight, expert_ids):
    dma = pltpu.SemaphoreType.DMA
    anywhere = pl.BlockSpec(memory_space=pl.ANY)
    ids = jnp.swapaxes(expert_ids, 1, 2)
    sums, wgrad = pl.pallas_call(
        kernel,
        out_shape=(
            jax.ShapeDtypeStruct((16, CW), BF16),
            jax.ShapeDtypeStruct((FL, D), BF16),
        ),
        in_specs=[anywhere] * 5,
        out_specs=(anywhere, anywhere),
        scratch_shapes=[
            pltpu.VMEM((4, D), BF16),
            pltpu.VMEM((FL, 128), BF16),
            pltpu.VMEM((FL, D), BF16),
            pltpu.VMEM((FL, D), BF16),
            pltpu.SMEM((2, 256), jnp.int32),
            pltpu.VMEM((2, Z, 2, 16, CW), BF16),
            pltpu.VMEM((8, 16, D), BF16),
            pltpu.VMEM((128, FL), F32),
            pltpu.VMEM((8, 16, D), BF16),
            pltpu.VMEM((FL, D), BF16),
            pltpu.VMEM((2, Z, 2, 16, CW), BF16),
            pltpu.VMEM((16, 2, 16, CW), BF16),
            pltpu.VMEM((16, 16, CW), BF16),
            pltpu.VMEM((16, 16, CW), BF16),
            pltpu.VMEM((16, 16, CW), F32),
            pltpu.VMEM((Z, 16, CW), BF16),
            pltpu.VMEM((Z, 16, CW), BF16),
            pltpu.VMEM((16, CW), BF16),
            dma((6,)),
            dma,
            dma((2, Z, 2)),
            dma((Z,)), dma((Z,)), dma((2 * Z,)),
            dma((Z,)), dma((Z,)),
            dma((Z,)), dma((Z,)),
            dma((Z,)), dma((Z,)),
            dma, dma,
        ],
        compiler_params=pltpu.CompilerParams(
            collective_id=0, has_side_effects=True, vmem_limit_bytes=60 * 2**20
        ),
        name="relay",
    )(
        layer_input,
        jnp.swapaxes(hidden_grad[0], 0, 1),
        jnp.swapaxes(gate_weight[0], 0, 1),
        jnp.swapaxes(up_weight[0], 0, 1),
        ids,
    )
    out, wgrad = pl.pallas_call(
        finish,
        out_shape=(
            jax.ShapeDtypeStruct((1, 4, D), BF16),
            jax.ShapeDtypeStruct((FL, D), BF16),
        ),
        in_specs=[anywhere] * 3,
        out_specs=(anywhere, anywhere),
        scratch_shapes=[
            pltpu.SMEM((2, 256), jnp.int32), pltpu.VMEM((16, CW), BF16), pltpu.VMEM((4, D), BF16),
            pltpu.VMEM((FL, D), BF16), dma((2 + PARTS,)), dma((1 + PARTS,)),
        ],
        compiler_params=pltpu.CompilerParams(vmem_limit_bytes=60 * 2**20),
        name="finish",
    )(ids, sums, wgrad)
    return out, jnp.swapaxes(wgrad, 0, 1)[None]


def solution(mesh):
    return jax.shard_map(
        per_device,
        mesh=mesh,
        in_specs=(
            P("section", "hid", None),
            P("section", None, "hid"),
            P("section", None, "hid"),
            P("section", None, "hid"),
            P(),
        ),
        out_specs=(P("section", "hid", None), P("section", None, "hid")),
        check_vma=False,
    )
```

```python
import functools

import jax
import jax.numpy as jnp
from jax import lax
from jax.experimental import pallas as pl
from jax.experimental.pallas import tpu as pltpu
from jax.sharding import PartitionSpec as P

MESH = pl.DeviceIdType.MESH
F32 = jnp.float32
BF16 = jnp.bfloat16
Z = 16
D = 4096
CH = 8
CW = D // CH
FL = 112
PARTS = 7

DISTANCES = tuple(range(1 - Z // 2, Z // 2 + 1))
FIRST, EACH, Y_TRIP, SLOT = 1.4, 0.6, 2.1, 0.28


def both_ways(tree):
    back = {-d: -p for d, p in tree.items() if d < Z // 2}
    return {**tree, **back}


GATHER_FROM = both_ways({1: 0, 2: 1, 3: 4, 4: 0, 5: 4, 6: 4, 7: 4, 8: 4})
SUM_FROM = both_ways({1: 0, 2: 0, 3: 0, 4: 2, 5: 2, 6: 0, 7: 6, 8: 6})


def trip(tree, d):
    return 0.0 if d == 0 else FIRST + EACH * abs(d - tree[d]) + trip(tree, tree[d])


def below(tree, d):
    return [c for c in tree if tree[c] == d]


def deepest(tree, d, top):
    return max([trip(tree, d)] + [deepest(tree, c, top) for c in below(tree, d)]) - (trip(tree, d) if top else 0.0)


def far_first(tree, d):
    return sorted(below(tree, d), key=lambda c: (-max(deepest(tree, c, False), trip(tree, c)), -abs(c), c))


GATHER_TO = {d: far_first(GATHER_FROM, d) for d in DISTANCES}
GATHER_ORDER = [
    (own, d)
    for _, own, d in sorted(
        [(trip(GATHER_FROM, d), True, d) for d in DISTANCES if d != 0]
        + [(trip(GATHER_FROM, d) + Y_TRIP, False, d) for d in DISTANCES]
    )
]
SUM_TO = {d: below(SUM_FROM, d) for d in DISTANCES}
SUM_Y_ORDER = sorted(DISTANCES, key=lambda d: (-trip(SUM_FROM, d), d))


def sum_ready(d):
    at = Y_TRIP + SLOT * SUM_Y_ORDER.index(d)
    return max([at] + [sum_ready(c) + FIRST + EACH * abs(c - d) for c in SUM_TO[d]])


SUM_Z_ORDER = sorted(DISTANCES, key=lambda d: (d == 0, sum_ready(d)))
LAST_ORDER = [d for d in SUM_Z_ORDER if SUM_FROM.get(d, 0) == 0]
REACH = sorted({s * (d - p) for d, p in GATHER_FROM.items() for s in (1, -1)})


def nt(left, right):
    return lax.dot_general(left, right, (((1,), (1,)), ((), ())), preferred_element_type=F32)


def nn(left, right):
    return lax.dot_general(left, right, (((1,), (0,)), ((), ())), preferred_element_type=F32)


def tn(left, right):
    return lax.dot_general(left, right, (((0,), (0,)), ((), ())), preferred_element_type=F32)


def iota(shape, dim):
    return lax.broadcasted_iota(jnp.int32, shape, dim)


def one_hot(mask):
    return jnp.where(mask, 1.0, 0.0).astype(BF16)


def piece_to_block(i):
    return (i % 8) * 16 + (i // 16) * 2 + (i // 8) % 2


def slots_of(ids_ref, hid_at):
    taken = jnp.int32(0)
    slots = []
    for t in range(4):
        chosen = jnp.where(ids_ref[0, hid_at * 4 + t] * ids_ref[1, hid_at * 4 + t] == 0, 1, 0)
        slots.append(jnp.where(chosen == 1, taken, -1))
        taken = taken + chosen
    return slots


def kernel(
    x_hbm, h_hbm, wg_hbm, wu_hbm, ids_hbm, got_out, wgrad_hbm,
    xs, hs, wg, wu, ids_a, got, rows, hid, part, wgrad,
    mine, core_in, y_out, y_in, acc, z_out, z_in, s5,
    load_sem, out_sem,
    got_r, gz_s, gy_s, gcore_s, c_s, c_r, y_s, y_r, z_s, z_r, give_sem, column_in,
):
    sec = lax.axis_index("section")
    n_sec = lax.axis_size("section")
    me = lax.axis_index("hid")
    core = me % 2
    z = (me // 2) % Z
    y = me // (2 * Z)
    prev_sec = (sec + n_sec - 1) % n_sec
    next_sec = (sec + 1) % n_sec

    def hid_of(y_at, z_at, core_at):
        return (y_at * Z + z_at) * 2 + core_at

    other_y = hid_of(1 - y, z, core)
    other_core = hid_of(y, z, 1 - core)

    def along(d):
        return (z + d + Z) % Z

    def loads(src, dst, i):
        return pltpu.make_async_copy(src, dst, load_sem.at[i])

    def remote(src, dst, send, recv, to, section=None):
        return pltpu.make_async_remote_copy(
            src_ref=src, dst_ref=dst, send_sem=send, recv_sem=recv,
            device_id={"section": sec if section is None else section, "hid": to},
            device_id_type=MESH,
        )

    load_ids = loads(ids_hbm.at[sec], ids_a, 0)
    load_x = loads(x_hbm.at[0], xs, 2)
    load_h = loads(h_hbm, hs, 3)
    load_wg = loads(wg_hbm, wg, 4)
    load_wu = loads(wu_hbm, wu, 5)
    for c in (load_ids, load_x, load_h, load_wg, load_wu):
        c.start()

    barrier = pltpu.get_barrier_semaphore()
    peers = [hid_of(y, along(d), core) for d in REACH] + [other_y, other_core]
    for p in peers:
        pl.semaphore_signal(barrier, inc=1, device_id={"section": sec, "hid": p}, device_id_type=MESH)
    pl.semaphore_signal(barrier, inc=1, device_id={"section": prev_sec, "hid": me}, device_id_type=MESH)

    load_ids.wait()
    load_x.wait()
    slots = slots_of(ids_a, me)
    row, tok = iota((16, 4), 0), iota((16, 4), 1)
    slot_of_tok = jnp.full((16, 4), -1, jnp.int32)
    for t in range(4):
        slot_of_tok = jnp.where(tok == t, slots[t], slot_of_tok)
    tok_rows = xs[...]
    piece = jnp.zeros((16, CW), F32)
    for j in range(CH):
        pick = one_hot((row // 8 == slot_of_tok) & (row % 8 == j))
        piece += nn(pick, tok_rows[:, j * CW:(j + 1) * CW])
    got[core, z, y] = piece.astype(BF16)

    pl.semaphore_wait(barrier, len(peers) + 1)

    sends = []

    def send(*a, **k):
        c = remote(*a, **k)
        c.start()
        sends.append(c)

    def pass_on(core_at, d, y_at, sem, to):
        ref = got.at[core_at, along(-d), y_at]
        return remote(ref, ref, sem, got_r.at[core_at, along(-d), y_at], to)

    def landed(core_at, d, y_at):
        pass_on(core_at, d, y_at, gcore_s.at[0], other_core).wait_recv()

    def send_on(copy):
        copy.start()
        sends.append(copy)

    def own_side(d):
        for to in GATHER_TO[d]:
            send_on(pass_on(core, d, y, gz_s.at[to + Z // 2 - 1], hid_of(y, along(to - d), core)))
        i = d + Z // 2 - 1
        send_on(pass_on(core, d, y, gy_s.at[i], other_y))
        send_on(pass_on(core, d, y, gcore_s.at[i], other_core))

    def other_side(d):
        landed(core, d, 1 - y)
        send_on(pass_on(core, d, 1 - y, gcore_s.at[Z + d + Z // 2 - 1], other_core))

    own_side(0)

    load_h.wait()
    m, o = iota((128, 128), 0), iota((128, 128), 1)
    slot_at = ((m // 16) % 2) * 64 + ((m // 32) % 2) * 32 + ((m // 2) % 8) * 4 + (m // 64) * 2 + m % 2
    hid[...] = nt(one_hot(o == slot_at), hs[...])

    for is_own, d in GATHER_ORDER:
        if is_own:
            landed(core, d, y)
            own_side(d)
        else:
            other_side(d)

    pl.semaphore_signal(column_in, inc=1, device_id={"section": next_sec, "hid": me}, device_id_type=MESH)
    to_block = one_hot(m == piece_to_block(o))

    def unpack(core_at):
        for o_z in range(2):
            for y_at in range(2):
                moved = nn(to_block, got[core_at, o_z * 8:o_z * 8 + 8, y_at].reshape(128, CW)).astype(BF16)
                b = (core_at * 2 + o_z) * 2 + y_at
                for j in range(CH):
                    rows[b, :, j * CW:(j + 1) * CW] = moved[j * 16:(j + 1) * 16]

    unpack(core)
    for d in DISTANCES:
        for y_at in range(2):
            landed(1 - core, d, y_at)
    unpack(1 - core)

    load_wg.wait()
    load_wu.wait()
    all_rows = rows[...].reshape(128, D)
    gate = nt(all_rows, wg[...])
    up = nt(all_rows, wu[...])
    sig = 1.0 / (1.0 + jnp.exp(-gate))
    hf = hid[...]
    d_gate = (hf * up * sig * (1.0 + gate * (1.0 - sig))).astype(BF16)
    d_up = (hf * gate * sig).astype(BF16)
    to_piece = one_hot(o == piece_to_block(m))
    part[...] = (nn(d_gate, wg[...]) + nn(d_up, wu[...])).astype(BF16).reshape(8, 16, D)

    def repack(core_at):
        for o_z in range(2):
            for y_at in range(2):
                own = part[(core_at * 2 + o_z) * 2 + y_at]
                stacked = jnp.concatenate([own[:, j * CW:(j + 1) * CW] for j in range(CH)], axis=0)
                moved = nn(to_piece, stacked).astype(BF16).reshape(8, 16, CW)
                mine[core_at, o_z * 8:o_z * 8 + 8, y_at] = moved

    def core_copy(i, d):
        return remote(mine.at[1 - core, along(-d)], core_in.at[i], c_s.at[i], c_r.at[i], other_core)

    def y_copy(i):
        return remote(y_out.at[i], y_in.at[i], y_s.at[i], y_r.at[i], other_y)

    def z_copy(d):
        i = d + Z // 2 - 1
        up = SUM_FROM.get(d, 0)
        section = prev_sec if up == 0 else sec
        return remote(z_out.at[i], z_in.at[i], z_s.at[i], z_r.at[i], hid_of(y, along(up - d), core), section)

    repack(1 - core)
    for i, d in enumerate(SUM_Y_ORDER):
        send_on(core_copy(i, d))
    repack(core)
    for i, d in enumerate(SUM_Y_ORDER):
        core_copy(i, d).wait_recv()
        at = along(-d)
        y_out[i] = (mine[core, at, 1 - y].astype(F32) + core_in[i, 1 - y].astype(F32)).astype(BF16)
        send_on(y_copy(i))
        acc[i] = mine[core, at, y].astype(F32) + core_in[i, y].astype(F32)
    told = False
    for d in SUM_Z_ORDER:
        i = SUM_Y_ORDER.index(d)
        y_copy(i).wait_recv()
        total = acc[i] + y_in[i].astype(F32)
        if d != 0:
            for child in SUM_TO[d]:
                z_copy(child).wait_recv()
                total += z_in[child + Z // 2 - 1].astype(F32)
        if SUM_FROM.get(d, 0) == 0 and not told:
            pl.semaphore_wait(column_in, 1)
            told = True
        z_out[d + Z // 2 - 1] = total.astype(BF16)
        send_on(z_copy(d))

    for j in range(CH):
        cols = slice(j * CW, (j + 1) * CW)
        wgrad[:, cols] = tn(d_gate, rows[:, :, cols].reshape(128, CW)).astype(BF16)
    store = pltpu.make_async_copy(wgrad, wgrad_hbm, out_sem)
    store.start()
    total = jnp.zeros((16, CW), F32)
    for child in LAST_ORDER:
        z_copy(child).wait_recv()
        total += z_in[child + Z // 2 - 1].astype(F32)
    s5[...] = total.astype(BF16)
    give = pltpu.make_async_copy(s5, got_out, give_sem)
    give.start()
    store.wait()
    for c in sends:
        c.wait_send()
    give.wait()


def finish(ids_hbm, got_hbm, wgrad_in, out_hbm, wgrad_out, ids, last_ref, tokens, held, sems, out_sems):
    me = lax.axis_index("hid")
    next_sec = (lax.axis_index("section") + 1) % lax.axis_size("section")
    load = pltpu.make_async_copy(ids_hbm.at[next_sec], ids, sems.at[0])
    load.start()
    load_last = pltpu.make_async_copy(got_hbm, last_ref, sems.at[1 + PARTS])
    load_last.start()
    step = FL // PARTS
    moves = []
    for i in range(PARTS):
        part = pl.ds(i * step, step)
        moves.append((
            pltpu.make_async_copy(wgrad_in.at[part], held.at[part], sems.at[1 + i]),
            pltpu.make_async_copy(held.at[part], wgrad_out.at[part], out_sems.at[i]),
        ))
        moves[-1][0].start()
    load.wait()
    slots = slots_of(ids, me)
    row, col = iota((4, 16), 0), iota((4, 16), 1)
    slot_of_row = jnp.full((4, 16), -1, jnp.int32)
    for t in range(4):
        slot_of_row = jnp.where(row == t, slots[t], slot_of_row)
    load_last.wait()
    last = last_ref[...]
    for j in range(CH):
        pick = one_hot((col // 8 == slot_of_row) & (col % 8 == j))
        tokens[:, j * CW:(j + 1) * CW] = nn(pick, last).astype(BF16)
    store = pltpu.make_async_copy(tokens, out_hbm.at[0], out_sems.at[PARTS])
    store.start()
    for come, go in moves:
        come.wait()
        go.start()
    for _, go in moves:
        go.wait()
    store.wait()


def per_device(layer_input, hidden_grad, gate_weight, up_weight, expert_ids):
    dma = pltpu.SemaphoreType.DMA
    anywhere = pl.BlockSpec(memory_space=pl.ANY)
    ids = jnp.swapaxes(expert_ids, 1, 2)
    sums, wgrad = pl.pallas_call(
        kernel,
        out_shape=(
            jax.ShapeDtypeStruct((16, CW), BF16),
            jax.ShapeDtypeStruct((FL, D), BF16),
        ),
        in_specs=[anywhere] * 5,
        out_specs=(anywhere, anywhere),
        scratch_shapes=[
            pltpu.VMEM((4, D), BF16),
            pltpu.VMEM((FL, 128), BF16),
            pltpu.VMEM((FL, D), BF16),
            pltpu.VMEM((FL, D), BF16),
            pltpu.SMEM((2, 256), jnp.int32),
            pltpu.VMEM((2, Z, 2, 16, CW), BF16),
            pltpu.VMEM((8, 16, D), BF16),
            pltpu.VMEM((128, FL), F32),
            pltpu.VMEM((8, 16, D), BF16),
            pltpu.VMEM((FL, D), BF16),
            pltpu.VMEM((2, Z, 2, 16, CW), BF16),
            pltpu.VMEM((16, 2, 16, CW), BF16),
            pltpu.VMEM((16, 16, CW), BF16),
            pltpu.VMEM((16, 16, CW), BF16),
            pltpu.VMEM((16, 16, CW), F32),
            pltpu.VMEM((Z, 16, CW), BF16),
            pltpu.VMEM((Z, 16, CW), BF16),
            pltpu.VMEM((16, CW), BF16),
            dma((6,)),
            dma,
            dma((2, Z, 2)),
            dma((Z,)), dma((Z,)), dma((2 * Z,)),
            dma((Z,)), dma((Z,)),
            dma((Z,)), dma((Z,)),
            dma((Z,)), dma((Z,)),
            dma, pltpu.SemaphoreType.REGULAR,
        ],
        compiler_params=pltpu.CompilerParams(
            collective_id=0, has_side_effects=True, vmem_limit_bytes=60 * 2**20
        ),
        name="relay",
    )(
        layer_input,
        jnp.swapaxes(hidden_grad[0], 0, 1),
        jnp.swapaxes(gate_weight[0], 0, 1),
        jnp.swapaxes(up_weight[0], 0, 1),
        ids,
    )
    out, wgrad = pl.pallas_call(
        finish,
        out_shape=(
            jax.ShapeDtypeStruct((1, 4, D), BF16),
            jax.ShapeDtypeStruct((FL, D), BF16),
        ),
        in_specs=[anywhere] * 3,
        out_specs=(anywhere, anywhere),
        scratch_shapes=[
            pltpu.SMEM((2, 256), jnp.int32), pltpu.VMEM((16, CW), BF16), pltpu.VMEM((4, D), BF16),
            pltpu.VMEM((FL, D), BF16), dma((2 + PARTS,)), dma((1 + PARTS,)),
        ],
        compiler_params=pltpu.CompilerParams(vmem_limit_bytes=60 * 2**20),
        name="finish",
    )(ids, sums, wgrad)
    return out, jnp.swapaxes(wgrad, 0, 1)[None]


def solution(mesh):
    return jax.shard_map(
        per_device,
        mesh=mesh,
        in_specs=(
            P("section", "hid", None),
            P("section", None, "hid"),
            P("section", None, "hid"),
            P("section", None, "hid"),
            P(),
        ),
        out_specs=(P("section", "hid", None), P("section", None, "hid")),
        check_vma=False,
    )
```

```python
import functools

import jax
import jax.numpy as jnp
from jax import lax
from jax.experimental import pallas as pl
from jax.experimental.pallas import tpu as pltpu
from jax.sharding import PartitionSpec as P

MESH = pl.DeviceIdType.MESH
F32 = jnp.float32
BF16 = jnp.bfloat16
Z = 16
D = 4096
CH = 8
CW = D // CH
FL = 112
PARTS = 7

DISTANCES = tuple(range(1 - Z // 2, Z // 2 + 1))
FIRST, EACH, Y_TRIP, SLOT = 1.4, 0.6, 3.0, 0.28


def both_ways(tree):
    back = {-d: -p for d, p in tree.items() if d < Z // 2}
    return {**tree, **back}


GATHER_FROM = both_ways({1: 0, 2: 1, 3: 4, 4: 0, 5: 4, 6: 4, 7: 4, 8: 4})
SUM_FROM = both_ways({1: 0, 2: 0, 3: 0, 4: 2, 5: 2, 6: 0, 7: 6, 8: 6})


def trip(tree, d):
    return 0.0 if d == 0 else FIRST + EACH * abs(d - tree[d]) + trip(tree, tree[d])


def below(tree, d):
    return [c for c in tree if tree[c] == d]


def deepest(tree, d, top):
    return max([trip(tree, d)] + [deepest(tree, c, top) for c in below(tree, d)]) - (trip(tree, d) if top else 0.0)


def far_first(tree, d):
    return sorted(below(tree, d), key=lambda c: (-max(deepest(tree, c, False), trip(tree, c)), -abs(c), c))


GATHER_TO = {d: far_first(GATHER_FROM, d) for d in DISTANCES}
GATHER_ORDER = [
    (own, d)
    for _, own, d in sorted(
        [(trip(GATHER_FROM, d), True, d) for d in DISTANCES if d != 0]
        + [(trip(GATHER_FROM, d) + Y_TRIP, False, d) for d in DISTANCES]
    )
]
SUM_TO = {d: below(SUM_FROM, d) for d in DISTANCES}
SUM_Y_ORDER = sorted(DISTANCES, key=lambda d: (-trip(SUM_FROM, d), d))


def sum_ready(d):
    at = Y_TRIP + SLOT * SUM_Y_ORDER.index(d)
    return max([at] + [sum_ready(c) + FIRST + EACH * abs(c - d) for c in SUM_TO[d]])


SUM_Z_ORDER = sorted(DISTANCES, key=lambda d: (d == 0, sum_ready(d)))
LAST_ORDER = [d for d in SUM_Z_ORDER if SUM_FROM.get(d, 0) == 0]
REACH = sorted({s * (d - p) for d, p in GATHER_FROM.items() for s in (1, -1)})


def nt(left, right):
    return lax.dot_general(left, right, (((1,), (1,)), ((), ())), preferred_element_type=F32)


def nn(left, right):
    return lax.dot_general(left, right, (((1,), (0,)), ((), ())), preferred_element_type=F32)


def tn(left, right):
    return lax.dot_general(left, right, (((0,), (0,)), ((), ())), preferred_element_type=F32)


def iota(shape, dim):
    return lax.broadcasted_iota(jnp.int32, shape, dim)


def one_hot(mask):
    return jnp.where(mask, 1.0, 0.0).astype(BF16)


def piece_to_block(i):
    return (i % 8) * 16 + (i // 16) * 2 + (i // 8) % 2


def slots_of(ids_ref, hid_at):
    taken = jnp.int32(0)
    slots = []
    for t in range(4):
        chosen = jnp.where(ids_ref[0, hid_at * 4 + t] * ids_ref[1, hid_at * 4 + t] == 0, 1, 0)
        slots.append(jnp.where(chosen == 1, taken, -1))
        taken = taken + chosen
    return slots


def kernel(
    x_hbm, h_hbm, wg_hbm, wu_hbm, ids_hbm, got_out, wgrad_hbm,
    xs, hs, wg, wu, ids_a, got, rows, hid, part, wgrad,
    mine, core_in, y_out, y_in, acc, z_out, z_in, s5,
    load_sem, out_sem,
    got_r, gz_s, gy_s, gcore_s, c_s, c_r, y_s, y_r, z_s, z_r, give_sem, column_in,
):
    sec = lax.axis_index("section")
    n_sec = lax.axis_size("section")
    me = lax.axis_index("hid")
    core = me % 2
    z = (me // 2) % Z
    y = me // (2 * Z)
    prev_sec = (sec + n_sec - 1) % n_sec
    next_sec = (sec + 1) % n_sec

    def hid_of(y_at, z_at, core_at):
        return (y_at * Z + z_at) * 2 + core_at

    other_y = hid_of(1 - y, z, core)
    other_core = hid_of(y, z, 1 - core)

    def along(d):
        return (z + d + Z) % Z

    def loads(src, dst, i):
        return pltpu.make_async_copy(src, dst, load_sem.at[i])

    def remote(src, dst, send, recv, to, section=None):
        return pltpu.make_async_remote_copy(
            src_ref=src, dst_ref=dst, send_sem=send, recv_sem=recv,
            device_id={"section": sec if section is None else section, "hid": to},
            device_id_type=MESH,
        )

    load_ids = loads(ids_hbm.at[sec], ids_a, 0)
    load_x = loads(x_hbm.at[0], xs, 2)
    load_h = loads(h_hbm, hs, 3)
    load_wg = loads(wg_hbm, wg, 4)
    load_wu = loads(wu_hbm, wu, 5)
    for c in (load_ids, load_x, load_h, load_wg, load_wu):
        c.start()

    barrier = pltpu.get_barrier_semaphore()
    peers = [hid_of(y, along(d), core) for d in REACH] + [other_y, other_core]
    for p in peers:
        pl.semaphore_signal(barrier, inc=1, device_id={"section": sec, "hid": p}, device_id_type=MESH)
    pl.semaphore_signal(barrier, inc=1, device_id={"section": prev_sec, "hid": me}, device_id_type=MESH)

    load_ids.wait()
    load_x.wait()
    slots = slots_of(ids_a, me)
    row, tok = iota((16, 4), 0), iota((16, 4), 1)
    slot_of_tok = jnp.full((16, 4), -1, jnp.int32)
    for t in range(4):
        slot_of_tok = jnp.where(tok == t, slots[t], slot_of_tok)
    tok_rows = xs[...]
    piece = jnp.zeros((16, CW), F32)
    for j in range(CH):
        pick = one_hot((row // 8 == slot_of_tok) & (row % 8 == j))
        piece += nn(pick, tok_rows[:, j * CW:(j + 1) * CW])
    got[core, z, y] = piece.astype(BF16)

    pl.semaphore_wait(barrier, len(peers) + 1)

    sends = []

    def send(*a, **k):
        c = remote(*a, **k)
        c.start()
        sends.append(c)

    def pass_on(core_at, d, y_at, sem, to):
        ref = got.at[core_at, along(-d), y_at]
        return remote(ref, ref, sem, got_r.at[core_at, along(-d), y_at], to)

    def landed(core_at, d, y_at):
        pass_on(core_at, d, y_at, gcore_s.at[0], other_core).wait_recv()

    def send_on(copy):
        copy.start()
        sends.append(copy)

    def own_side(d):
        for to in GATHER_TO[d]:
            send_on(pass_on(core, d, y, gz_s.at[to + Z // 2 - 1], hid_of(y, along(to - d), core)))
        i = d + Z // 2 - 1
        send_on(pass_on(core, d, y, gy_s.at[i], other_y))
        send_on(pass_on(core, d, y, gcore_s.at[i], other_core))

    def other_side(d):
        landed(core, d, 1 - y)
        send_on(pass_on(core, d, 1 - y, gcore_s.at[Z + d + Z // 2 - 1], other_core))

    own_side(0)

    load_h.wait()
    m, o = iota((128, 128), 0), iota((128, 128), 1)
    slot_at = ((m // 16) % 2) * 64 + ((m // 32) % 2) * 32 + ((m // 2) % 8) * 4 + (m // 64) * 2 + m % 2
    hid[...] = nt(one_hot(o == slot_at), hs[...])

    for is_own, d in GATHER_ORDER:
        if is_own:
            landed(core, d, y)
            own_side(d)
        else:
            other_side(d)

    pl.semaphore_signal(column_in, inc=1, device_id={"section": next_sec, "hid": me}, device_id_type=MESH)
    to_block = one_hot(m == piece_to_block(o))

    def unpack(core_at):
        for o_z in range(2):
            for y_at in range(2):
                moved = nn(to_block, got[core_at, o_z * 8:o_z * 8 + 8, y_at].reshape(128, CW)).astype(BF16)
                b = (core_at * 2 + o_z) * 2 + y_at
                for j in range(CH):
                    rows[b, :, j * CW:(j + 1) * CW] = moved[j * 16:(j + 1) * 16]

    unpack(core)
    for d in DISTANCES:
        for y_at in range(2):
            landed(1 - core, d, y_at)
    unpack(1 - core)

    load_wg.wait()
    load_wu.wait()
    all_rows = rows[...].reshape(128, D)
    gate = nt(all_rows, wg[...])
    up = nt(all_rows, wu[...])
    sig = 1.0 / (1.0 + jnp.exp(-gate))
    hf = hid[...]
    d_gate = (hf * up * sig * (1.0 + gate * (1.0 - sig))).astype(BF16)
    d_up = (hf * gate * sig).astype(BF16)
    to_piece = one_hot(o == piece_to_block(m))
    part[...] = (nn(d_gate, wg[...]) + nn(d_up, wu[...])).astype(BF16).reshape(8, 16, D)

    def repack(core_at):
        for o_z in range(2):
            for y_at in range(2):
                own = part[(core_at * 2 + o_z) * 2 + y_at]
                stacked = jnp.concatenate([own[:, j * CW:(j + 1) * CW] for j in range(CH)], axis=0)
                moved = nn(to_piece, stacked).astype(BF16).reshape(8, 16, CW)
                mine[core_at, o_z * 8:o_z * 8 + 8, y_at] = moved

    def core_copy(i, d):
        return remote(mine.at[1 - core, along(-d)], core_in.at[i], c_s.at[i], c_r.at[i], other_core)

    def y_copy(i):
        return remote(y_out.at[i], y_in.at[i], y_s.at[i], y_r.at[i], other_y)

    def z_copy(d):
        i = d + Z // 2 - 1
        up = SUM_FROM.get(d, 0)
        section = prev_sec if up == 0 else sec
        return remote(z_out.at[i], z_in.at[i], z_s.at[i], z_r.at[i], hid_of(y, along(up - d), core), section)

    repack(1 - core)
    for i, d in enumerate(SUM_Y_ORDER):
        send_on(core_copy(i, d))
    repack(core)
    for i, d in enumerate(SUM_Y_ORDER):
        core_copy(i, d).wait_recv()
        at = along(-d)
        y_out[i] = (mine[core, at, 1 - y].astype(F32) + core_in[i, 1 - y].astype(F32)).astype(BF16)
        send_on(y_copy(i))
        acc[i] = mine[core, at, y].astype(F32) + core_in[i, y].astype(F32)
    told = False
    for d in SUM_Z_ORDER:
        i = SUM_Y_ORDER.index(d)
        y_copy(i).wait_recv()
        total = acc[i] + y_in[i].astype(F32)
        if d != 0:
            for child in SUM_TO[d]:
                z_copy(child).wait_recv()
                total += z_in[child + Z // 2 - 1].astype(F32)
        if SUM_FROM.get(d, 0) == 0 and not told:
            pl.semaphore_wait(column_in, 1)
            told = True
        z_out[d + Z // 2 - 1] = total.astype(BF16)
        send_on(z_copy(d))

    for j in range(CH):
        cols = slice(j * CW, (j + 1) * CW)
        wgrad[:, cols] = tn(d_gate, rows[:, :, cols].reshape(128, CW)).astype(BF16)
    store = pltpu.make_async_copy(wgrad, wgrad_hbm, out_sem)
    store.start()
    for c in sends:
        c.wait_send()
    total = jnp.zeros((16, CW), F32)
    for child in LAST_ORDER:
        z_copy(child).wait_recv()
        total += z_in[child + Z // 2 - 1].astype(F32)
    s5[...] = total.astype(BF16)
    give = pltpu.make_async_copy(s5, got_out, give_sem)
    give.start()
    store.wait()
    give.wait()


def finish(ids_hbm, got_hbm, wgrad_in, out_hbm, wgrad_out, ids, last_ref, tokens, held, sems, out_sems):
    me = lax.axis_index("hid")
    next_sec = (lax.axis_index("section") + 1) % lax.axis_size("section")
    load = pltpu.make_async_copy(ids_hbm.at[next_sec], ids, sems.at[0])
    load.start()
    load_last = pltpu.make_async_copy(got_hbm, last_ref, sems.at[1 + PARTS])
    load_last.start()
    step = FL // PARTS
    moves = []
    for i in range(PARTS):
        part = pl.ds(i * step, step)
        moves.append((
            pltpu.make_async_copy(wgrad_in.at[part], held.at[part], sems.at[1 + i]),
            pltpu.make_async_copy(held.at[part], wgrad_out.at[part], out_sems.at[i]),
        ))
        moves[-1][0].start()
    load.wait()
    slots = slots_of(ids, me)
    row, col = iota((4, 16), 0), iota((4, 16), 1)
    slot_of_row = jnp.full((4, 16), -1, jnp.int32)
    for t in range(4):
        slot_of_row = jnp.where(row == t, slots[t], slot_of_row)
    load_last.wait()
    last = last_ref[...]
    for j in range(CH):
        pick = one_hot((col // 8 == slot_of_row) & (col % 8 == j))
        tokens[:, j * CW:(j + 1) * CW] = nn(pick, last).astype(BF16)
    store = pltpu.make_async_copy(tokens, out_hbm.at[0], out_sems.at[PARTS])
    store.start()
    for come, go in moves:
        come.wait()
        go.start()
    for _, go in moves:
        go.wait()
    store.wait()


def per_device(layer_input, hidden_grad, gate_weight, up_weight, expert_ids):
    dma = pltpu.SemaphoreType.DMA
    anywhere = pl.BlockSpec(memory_space=pl.ANY)
    ids = jnp.swapaxes(expert_ids, 1, 2)
    sums, wgrad = pl.pallas_call(
        kernel,
        out_shape=(
            jax.ShapeDtypeStruct((16, CW), BF16),
            jax.ShapeDtypeStruct((FL, D), BF16),
        ),
        in_specs=[anywhere] * 5,
        out_specs=(anywhere, anywhere),
        scratch_shapes=[
            pltpu.VMEM((4, D), BF16),
            pltpu.VMEM((FL, 128), BF16),
            pltpu.VMEM((FL, D), BF16),
            pltpu.VMEM((FL, D), BF16),
            pltpu.SMEM((2, 256), jnp.int32),
            pltpu.VMEM((2, Z, 2, 16, CW), BF16),
            pltpu.VMEM((8, 16, D), BF16),
            pltpu.VMEM((128, FL), F32),
            pltpu.VMEM((8, 16, D), BF16),
            pltpu.VMEM((FL, D), BF16),
            pltpu.VMEM((2, Z, 2, 16, CW), BF16),
            pltpu.VMEM((16, 2, 16, CW), BF16),
            pltpu.VMEM((16, 16, CW), BF16),
            pltpu.VMEM((16, 16, CW), BF16),
            pltpu.VMEM((16, 16, CW), F32),
            pltpu.VMEM((Z, 16, CW), BF16),
            pltpu.VMEM((Z, 16, CW), BF16),
            pltpu.VMEM((16, CW), BF16),
            dma((6,)),
            dma,
            dma((2, Z, 2)),
            dma((Z,)), dma((Z,)), dma((2 * Z,)),
            dma((Z,)), dma((Z,)),
            dma((Z,)), dma((Z,)),
            dma((Z,)), dma((Z,)),
            dma, pltpu.SemaphoreType.REGULAR,
        ],
        compiler_params=pltpu.CompilerParams(
            collective_id=0, has_side_effects=True, vmem_limit_bytes=60 * 2**20
        ),
        name="relay",
    )(
        layer_input,
        jnp.swapaxes(hidden_grad[0], 0, 1),
        jnp.swapaxes(gate_weight[0], 0, 1),
        jnp.swapaxes(up_weight[0], 0, 1),
        ids,
    )
    out, wgrad = pl.pallas_call(
        finish,
        out_shape=(
            jax.ShapeDtypeStruct((1, 4, D), BF16),
            jax.ShapeDtypeStruct((FL, D), BF16),
        ),
        in_specs=[anywhere] * 3,
        out_specs=(anywhere, anywhere),
        scratch_shapes=[
            pltpu.SMEM((2, 256), jnp.int32), pltpu.VMEM((16, CW), BF16), pltpu.VMEM((4, D), BF16),
            pltpu.VMEM((FL, D), BF16), dma((2 + PARTS,)), dma((1 + PARTS,)),
        ],
        compiler_params=pltpu.CompilerParams(vmem_limit_bytes=60 * 2**20),
        name="finish",
    )(ids, sums, wgrad)
    return out, jnp.swapaxes(wgrad, 0, 1)[None]


def solution(mesh):
    return jax.shard_map(
        per_device,
        mesh=mesh,
        in_specs=(
            P("section", "hid", None),
            P("section", None, "hid"),
            P("section", None, "hid"),
            P("section", None, "hid"),
            P(),
        ),
        out_specs=(P("section", "hid", None), P("section", None, "hid")),
        check_vma=False,
    )
```
